32 devices in a mesh: grp: 2 (over y), mode: 4 (over z), site: 4 (over x, core).
Axes of the slice: x: 2, y: 2, z: 4, core: 2. Of those that a mesh axis runs over, the one named last changes fastest.
Arguments:
- w_modes: bfloat16 [2, 1024, 12, 256], P(None, ('grp', 'mode'), None, 'site'), parts along dimension 1, may hold values from -6 to 6
- v_modes: bfloat16 [2, 512, 12, 256], P(None, ('grp', 'mode'), None, 'site'), parts along dimension 1, may hold values from -0.078125 to 0.078125
- momenta: int32 [4, 3], replicated, may hold values from -2 to 2
Outputs:
- meson: float32 [2, 4, 1024, 192], P(None, None, ('grp', 'mode', 'site')), parts along dimension 2
The draws below stay inside these ranges and needn't reach their ends.
There are 2 independent parts, one for each index of `grp`. The reference program is written for one: setup_inputs(seed, part) draws one part's arguments, and reference() takes and returns one part's arrays. A program takes and returns all parts, laid end to end along the dimension named above; an argument that names none is the same for every part. Nothing has to cross between parts.
All inputs are finite; a program needn't handle non-finite values.
Results may differ from the reference program's by a relative error of at most 0.0028.
Values may be sent and summed in bfloat16 or wider, within the bound.
No kernel may reach another device: no remote copies, remote signals or barrier semaphores. Data moves between devices by JAX's collectives and lax.ppermute only.
A program may use at most 64 MiB of HBM per device.

```python
import jax
import jax.numpy as jnp
import numpy as np
from jax import lax

W_DEV = 128
VB = 64
NPH = 4
LAT = 96
STEPS = 1
NW = 512
NV = 256
SITES = 256


def with_ends(drawn, stream_key, low, top_value):
    spot = [jax.random.randint(jax.random.fold_in(stream_key, axis), (), 0, length) for axis, length in enumerate(drawn.shape)]
    main_axis = drawn.shape.index(max(drawn.shape))
    beside = spot[:main_axis] + [(spot[main_axis] + 1) % drawn.shape[main_axis]] + spot[main_axis + 1:]
    return drawn.at[tuple(spot)].set(low).at[tuple(beside)].set(top_value)


def shard_levels(own_key, extent, cuts, smallest, high):
    gain = 1.0
    for position, shards_of in cuts:
        steps = jax.random.uniform(jax.random.fold_in(jax.random.fold_in(own_key, 6), position), (shards_of,), jnp.float32, smallest / len(cuts), high / len(cuts))
        gain = gain * jnp.repeat(jnp.exp(steps), extent[position] // shards_of).reshape((-1,) + (1,) * (len(extent) - 1 - position))
    return gain


def noise(key, extent, deviation, limit, shards=(), kind=jnp.bfloat16):
    result = deviation * jax.random.normal(key, extent, jnp.float32)
    if shards:
        result = result * shard_levels(key, extent, shards, -0.22, 0.18)
    return jnp.clip(result, -limit, limit).astype(kind)


def setup_inputs(seed: int = 0, part: int = 0) -> dict:
    seeds = jax.random.split(jax.random.key(seed), 4)
    own_keys = jax.random.split(jax.random.fold_in(seeds[3], part), 4)
    w_modes = noise(own_keys[0], (2, NW, 12, SITES), 1.0, 6.0, ((1, 4), (3, 4)))
    v_modes = noise(own_keys[1], (2, NV, 12, SITES), (24 * SITES) ** -0.5, 0.078125, ((1, 4), (3, 4)))
    momenta = with_ends(jax.random.randint(seeds[2], (NPH, 3), -2, 3), jax.random.fold_in(seeds[2], 1), -2, 2).astype(jnp.int32)
    return {"w_modes": w_modes, "v_modes": v_modes, "momenta": momenta}


def make_phase(momenta, first, count):
    index = first + jnp.arange(count, dtype=jnp.int32)
    xcoord = index % LAT
    ycoord = (index // LAT) % LAT
    zcoord = index // (LAT * LAT)
    total = momenta[:, 0:1] * xcoord[None, :] + momenta[:, 1:2] * ycoord[None, :] + momenta[:, 2:3] * zcoord[None, :]
    wound = total % LAT
    angle = (-2.0 * np.pi / LAT) * wound.astype(jnp.float32)
    return jnp.cos(angle), jnp.sin(angle)


def apply_gamma(vectors):
    count = vectors.shape[1]
    sites = vectors.shape[3]
    shaped = vectors.reshape(2, count, 4, 3, sites)
    signs = jnp.array([-1.0, 1.0, 1.0, -1.0], jnp.float32)
    flipped = shaped[:, :, ::-1].astype(jnp.float32) * signs[None, None, :, None, None]
    return flipped.astype(jnp.bfloat16).reshape(2, count, 12, sites)


def phased_rows(wblock, cosine, sine):
    wreal = wblock[0].astype(jnp.float32)
    wimag = wblock[1].astype(jnp.float32)
    creal = cosine[:, None, None, :]
    cimag = sine[:, None, None, :]
    areal = wreal[None] * creal + wimag[None] * cimag
    aimag = wreal[None] * cimag - wimag[None] * creal
    rows = areal.shape[0] * areal.shape[1]
    width = areal.shape[2] * areal.shape[3]
    return jnp.concatenate([areal.reshape(rows, width), aimag.reshape(rows, width)], axis=0).astype(jnp.bfloat16)


def reference(w_modes, v_modes, momenta):
    nmode = w_modes.shape[1] // W_DEV
    sites = w_modes.shape[3]
    cosine, sine = make_phase(momenta, 0, sites)
    gv = apply_gamma(v_modes).reshape(2, nmode, VB, 12, sites)
    width = 12 * sites
    nblocks = 2 * STEPS + 1
    nband = nblocks * VB

    def one_owner(owner):
        wblock = lax.dynamic_slice_in_dim(w_modes, (owner * W_DEV).astype(jnp.int32), W_DEV, 1)
        lhs = phased_rows(wblock, cosine, sine).astype(jnp.float32)
        picks = ((owner + jnp.arange(nblocks, dtype=jnp.int32) - STEPS) % nmode).astype(jnp.int32)
        band = jnp.take(gv, picks, axis=1).reshape(2, nband, width)
        rhs = jnp.concatenate([band[0], band[1]], axis=0).astype(jnp.float32)
        prod = lax.dot_general(lhs, rhs, (((1,), (1,)), ((), ())), preferred_element_type=jnp.float32)
        half_rows = NPH * W_DEV
        real_part = prod[:half_rows, :nband] - prod[half_rows:, nband:]
        imag_part = prod[:half_rows, nband:] + prod[half_rows:, :nband]
        return jnp.stack([real_part, imag_part]).reshape(2, NPH, W_DEV, nband)

    owners = jnp.arange(nmode, dtype=jnp.int32)
    stacked = lax.map(one_owner, owners)
    return jnp.transpose(stacked, (1, 2, 0, 3, 4)).reshape(2, NPH, nmode * W_DEV, nband)
```

```python
import jax
import jax.numpy as jnp
import numpy as np
from jax import lax
from jax.experimental import pallas as pl
from jax.experimental.pallas import tpu as pltpu
from jax.sharding import PartitionSpec as P

LAT = 96
REACH = 4
SPINS = 4
SIGNS = (-1.0, 1.0, 1.0, -1.0)


def shifted(value, axis, steps):
    count = lax.axis_size(axis)
    pairs = [(source, (source + steps) % count) for source in range(count)]
    return lax.ppermute(value, axis, pairs)


def peer(index, slot, count):
    if count & (count - 1) == 0:
        return index ^ slot
    return (index + slot) % count


def traded(value, axis, slot):
    count = lax.axis_size(axis)
    pairs = [(source, peer(source, slot, count)) for source in range(count)]
    return lax.ppermute(value, axis, pairs)


def make_phase(momenta, first, count):
    index = first + jnp.arange(count, dtype=jnp.int32)
    xcoord = index % LAT
    ycoord = index // LAT % LAT
    zcoord = index // (LAT * LAT)
    total = (
        momenta[:, 0:1] * xcoord[None, :]
        + momenta[:, 1:2] * ycoord[None, :]
        + momenta[:, 2:3] * zcoord[None, :]
    )
    wound = total % LAT
    angle = -2.0 * np.pi / LAT * wound.astype(jnp.float32)
    return (jnp.cos(angle), jnp.sin(angle))


def prepare_kernel(slots, nph, rows, owner_ref, w_ref, cos_ref, sin_ref, b_ref):
    wrows = w_ref.shape[3]
    sites = w_ref.shape[2]
    nsc = w_ref.shape[1]
    colours = nsc // SPINS
    wide = nph * rows
    lane = lax.broadcasted_iota(jnp.int32, (wrows, wide), 1) % rows
    line = lax.broadcasted_iota(jnp.int32, (wrows, wide), 0)
    picks = jnp.concatenate(
        [(line == lane + owner_ref[slot] * rows).astype(jnp.float32) for slot in range(slots)], axis=1
    ).astype(jnp.bfloat16)
    cosine = cos_ref[...]
    sine = sin_ref[...]
    for sc in range(nsc):
        spin, colour = divmod(sc, colours)
        other = (SPINS - 1 - spin) * colours + colour
        c, s = (cosine, sine) if SIGNS[SPINS - 1 - spin] > 0 else (-cosine, -sine)
        both = jnp.concatenate([w_ref[0, other], w_ref[1, other]], axis=0)
        spread = jnp.dot(both, picks, preferred_element_type=jnp.float32)
        for slot in range(slots):
            wreal = spread[:sites, slot * wide : (slot + 1) * wide]
            wimag = spread[sites:, slot * wide : (slot + 1) * wide]
            areal = wreal * c + wimag * s
            aimag = wreal * s - wimag * c
            low = areal.astype(jnp.bfloat16)
            high = aimag.astype(jnp.bfloat16)
            top = slice(sc * 2 * sites, (sc * 2 + 1) * sites)
            bottom = slice((sc * 2 + 1) * sites, (sc * 2 + 2) * sites)
            first = slice((2 * slot) * wide, (2 * slot + 1) * wide)
            second = slice((2 * slot + 1) * wide, (2 * slot + 2) * wide)
            b_ref[top, first] = low
            b_ref[bottom, first] = (-aimag).astype(jnp.bfloat16)
            b_ref[top, second] = high
            b_ref[bottom, second] = low


def contract_kernel(count, slots, *refs):
    blocks = refs[:count]
    b_ref = refs[count]
    outs = refs[count + 1 :]
    nsc = blocks[0].shape[0]
    vrows = blocks[0].shape[1]
    lhs = jnp.concatenate(
        [jnp.concatenate([block[sc] for sc in range(nsc)], axis=1) for block in blocks], axis=0
    )
    width = b_ref.shape[1] // slots
    for slot in range(slots):
        part = jnp.dot(lhs, b_ref[:, slot * width : (slot + 1) * width], preferred_element_type=jnp.float32)
        outs[slot][...] = part.astype(outs[slot].dtype)


def finish_kernel(order, groups, slots, vrows, *refs):
    out_ref = refs[-1]
    sums = []
    for group in range(groups):
        parts = refs[group * slots : (group + 1) * slots]
        total = parts[0][...]
        for part in parts[1:]:
            total = total + part[...].astype(jnp.float32)
        sums.append(total)
    band = [sums[group][row * vrows : (row + 1) * vrows] for group, row in order]
    out_ref[...] = jnp.concatenate(band, axis=0).T


VMEM = pl.BlockSpec(memory_space=pltpu.VMEM)
GRANT = 16 << 20


def local_call(body, name, out_shape, in_specs, flops, *operands):
    outs = out_shape if isinstance(out_shape, list) else [out_shape]
    moved = sum(int(np.prod(x.shape)) * x.dtype.itemsize for x in [*operands, *outs])
    return pl.pallas_call(
        body,
        out_shape=out_shape,
        in_specs=in_specs,
        out_specs=[VMEM] * len(outs) if isinstance(out_shape, list) else VMEM,
        name=name,
        cost_estimate=pl.CostEstimate(flops=flops, bytes_accessed=moved, transcendentals=0),
        compiler_params=pltpu.CompilerParams(vmem_limit_bytes=GRANT),
    )(*operands)


def shards(w_modes, v_modes, momenta):
    wrows = w_modes.shape[1]
    nsc = w_modes.shape[2]
    sites = w_modes.shape[3]
    vrows = v_modes.shape[1]
    nph = momenta.shape[0]
    nmode = lax.axis_size("mode")
    nsite = lax.axis_size("site")
    reach = min(REACH, (nmode - 1) // 2)
    rows = wrows // nsite
    width = 2 * nph * rows
    me = lax.axis_index("site")

    vt = jnp.transpose(v_modes, (0, 2, 1, 3))
    packed = jnp.concatenate([vt[0], vt[1]], axis=-1)
    offsets = [sign * step for step in range(1, reach + 1) for sign in (1, -1)]
    arrived = [shifted(packed, "mode", -offset) for offset in offsets]

    cosine, sine = make_phase(momenta, me * sites, sites)
    cosine = jnp.repeat(cosine.T, rows, axis=1)
    sine = jnp.repeat(sine.T, rows, axis=1)
    owners = jnp.stack([peer(me, slot, nsite) for slot in range(nsite)]).astype(jnp.int32)
    wt = jnp.transpose(w_modes, (0, 2, 3, 1))
    rhs = local_call(
        lambda *refs: prepare_kernel(nsite, nph, rows, *refs),
        "prepare",
        jax.ShapeDtypeStruct((nsc * 2 * sites, nsite * width), jnp.bfloat16),
        [pl.BlockSpec(memory_space=pltpu.SMEM), VMEM, VMEM, VMEM],
        2 * nsc * 2 * sites * wrows * nsite * nph * rows,
        owners,
        wt,
        cosine,
        sine,
    )

    def group_of(blocks):
        shape = (len(blocks) * vrows, width)
        parts = local_call(
            lambda *refs: contract_kernel(len(blocks), nsite, *refs),
            "contract",
            [jax.ShapeDtypeStruct(shape, jnp.float32)]
            + [jax.ShapeDtypeStruct(shape, jnp.bfloat16)] * (nsite - 1),
            [VMEM] * (len(blocks) + 1),
            2 * shape[0] * rhs.shape[0] * rhs.shape[1],
            *blocks,
            rhs,
        )
        return [parts[0]] + [traded(parts[slot], "site", slot) for slot in range(1, nsite)]

    first = group_of([packed])
    rest = group_of(arrived)
    place = {0: (0, 0)}
    for row, offset in enumerate(offsets):
        place[offset] = (1, row)
    order = [place[offset] for offset in range(-reach, reach + 1)]
    out = local_call(
        lambda *refs: finish_kernel(order, 2, nsite, vrows, *refs),
        "finish",
        jax.ShapeDtypeStruct((width, len(order) * vrows), jnp.float32),
        [VMEM] * (2 * nsite),
        0,
        *first,
        *rest,
    )
    return out.reshape(2, nph, rows, len(order) * vrows)


def solution(mesh):
    placed = (P(None, ("grp", "mode"), None, "site"), P(None, ("grp", "mode"), None, "site"), P())
    return jax.shard_map(
        shards,
        mesh=mesh,
        in_specs=placed,
        out_specs=P(None, None, ("grp", "mode", "site"), None),
        check_vma=False,
    )
```

```python
import jax
import jax.numpy as jnp
import numpy as np
from jax import lax
from jax.experimental import pallas as pl
from jax.experimental.pallas import tpu as pltpu
from jax.sharding import PartitionSpec as P

LAT = 96
REACH = 4
SPINS = 4
SIGNS = (-1.0, 1.0, 1.0, -1.0)


def shifted(value, axis, steps):
    count = lax.axis_size(axis)
    pairs = [(source, (source + steps) % count) for source in range(count)]
    return lax.ppermute(value, axis, pairs)


def traded(value, axis, distance):
    count = lax.axis_size(axis)
    return lax.ppermute(value, axis, [(source, source ^ distance) for source in range(count)])


def slot_order(count):
    order = [0]
    distance = count // 2
    while distance:
        order = order + [slot + distance for slot in order]
        distance //= 2
    return order


def make_phase(momenta, first, count):
    index = first + jnp.arange(count, dtype=jnp.int32)
    xcoord = index % LAT
    ycoord = index // LAT % LAT
    zcoord = index // (LAT * LAT)
    total = (
        momenta[:, 0:1] * xcoord[None, :]
        + momenta[:, 1:2] * ycoord[None, :]
        + momenta[:, 2:3] * zcoord[None, :]
    )
    wound = total % LAT
    angle = -2.0 * np.pi / LAT * wound.astype(jnp.float32)
    return (jnp.cos(angle), jnp.sin(angle))


def prepare_kernel(slots, nph, rows, owner_ref, w_ref, cos_ref, sin_ref, b_ref):
    wrows = w_ref.shape[3]
    sites = w_ref.shape[2]
    nsc = w_ref.shape[1]
    colours = nsc // SPINS
    wide = nph * rows
    lane = lax.broadcasted_iota(jnp.int32, (wrows, wide), 1) % rows
    line = lax.broadcasted_iota(jnp.int32, (wrows, wide), 0)
    picks = jnp.concatenate(
        [(line == lane + owner_ref[slot] * rows).astype(jnp.float32) for slot in range(slots)], axis=1
    ).astype(jnp.bfloat16)
    cosine = cos_ref[...]
    sine = sin_ref[...]
    for sc in range(nsc):
        spin, colour = divmod(sc, colours)
        other = (SPINS - 1 - spin) * colours + colour
        c, s = (cosine, sine) if SIGNS[SPINS - 1 - spin] > 0 else (-cosine, -sine)
        both = jnp.concatenate([w_ref[0, other], w_ref[1, other]], axis=0)
        spread = jnp.dot(both, picks, preferred_element_type=jnp.float32)
        for slot in range(slots):
            wreal = spread[:sites, slot * wide : (slot + 1) * wide]
            wimag = spread[sites:, slot * wide : (slot + 1) * wide]
            areal = wreal * c + wimag * s
            aimag = wreal * s - wimag * c
            low = areal.astype(jnp.bfloat16)
            high = aimag.astype(jnp.bfloat16)
            top = slice(sc * 2 * sites, (sc * 2 + 1) * sites)
            bottom = slice((sc * 2 + 1) * sites, (sc * 2 + 2) * sites)
            first = slice((2 * slot) * wide, (2 * slot + 1) * wide)
            second = slice((2 * slot + 1) * wide, (2 * slot + 2) * wide)
            b_ref[top, first] = low
            b_ref[bottom, first] = (-aimag).astype(jnp.bfloat16)
            b_ref[top, second] = high
            b_ref[bottom, second] = low


def contract_kernel(*refs):
    *blocks, b_ref, keep_ref, send_ref = refs
    lhs = jnp.concatenate(
        [jnp.concatenate([block[sc] for sc in range(block.shape[0])], axis=1) for block in blocks], axis=0
    )
    width = keep_ref.shape[1]
    for out, first in ((send_ref, width), (keep_ref, 0)):
        part = jnp.dot(lhs, b_ref[:, first : first + width], preferred_element_type=jnp.float32)
        out[...] = part.astype(out.dtype)


def total_of(kept, came):
    return kept[...] + came[...].astype(jnp.float32)


def combine_kernel(kept_ref, came_ref, keep_ref, send_ref):
    total = total_of(kept_ref, came_ref)
    width = keep_ref.shape[1]
    send_ref[...] = total[:, width:].astype(send_ref.dtype)
    keep_ref[...] = total[:, :width]


def gather_kernel(*refs):
    *parts, out_ref = refs
    sums = [total_of(*parts[at : at + 2]) for at in range(0, len(parts), 2)]
    out_ref[...] = jnp.concatenate(sums, axis=0).T


def finish_kernel(near_ref, kept_ref, came_ref, out_ref):
    out_ref[...] = jnp.concatenate([near_ref[...], total_of(kept_ref, came_ref).T], axis=1)


VMEM = pl.BlockSpec(memory_space=pltpu.VMEM)
GRANT = 16 << 20


def local_call(body, name, out_shape, in_specs, flops, *operands):
    outs = out_shape if isinstance(out_shape, list) else [out_shape]
    moved = sum(int(np.prod(x.shape)) * x.dtype.itemsize for x in [*operands, *outs])
    return pl.pallas_call(
        body,
        out_shape=out_shape,
        in_specs=in_specs,
        out_specs=[VMEM] * len(outs) if isinstance(out_shape, list) else VMEM,
        name=name,
        cost_estimate=pl.CostEstimate(flops=flops, bytes_accessed=moved, transcendentals=0),
        compiler_params=pltpu.CompilerParams(vmem_limit_bytes=GRANT),
    )(*operands)


def shards(w_modes, v_modes, momenta):
    wrows = w_modes.shape[1]
    nsc = w_modes.shape[2]
    sites = w_modes.shape[3]
    vrows = v_modes.shape[1]
    nph = momenta.shape[0]
    nmode = lax.axis_size("mode")
    nsite = lax.axis_size("site")
    reach = min(REACH, (nmode - 1) // 2)
    rows = wrows // nsite
    width = 2 * nph * rows
    me = lax.axis_index("site")

    vt = jnp.transpose(v_modes, (0, 2, 1, 3))
    packed = jnp.concatenate([vt[0], vt[1]], axis=-1)
    below = [shifted(packed, "mode", step) for step in range(reach, 0, -1)]
    above = [shifted(packed, "mode", -step) for step in range(1, reach + 1)]

    cosine, sine = make_phase(momenta, me * sites, sites)
    cosine = jnp.repeat(cosine.T, rows, axis=1)
    sine = jnp.repeat(sine.T, rows, axis=1)
    owners = jnp.stack([me ^ slot for slot in slot_order(nsite)]).astype(jnp.int32)
    wt = jnp.transpose(w_modes, (0, 2, 3, 1))
    rhs = local_call(
        lambda *refs: prepare_kernel(nsite, nph, rows, *refs),
        "prepare",
        jax.ShapeDtypeStruct((nsc * 2 * sites, nsite * width), jnp.bfloat16),
        [pl.BlockSpec(memory_space=pltpu.SMEM), VMEM, VMEM, VMEM],
        2 * nsc * 2 * sites * wrows * nsite * nph * rows,
        owners,
        wt,
        cosine,
        sine,
    )

    def group_of(blocks):
        height = len(blocks) * vrows
        columns = nsite * width // 2
        keep, send = local_call(
            contract_kernel,
            "contract",
            [jax.ShapeDtypeStruct((height, columns), jnp.float32)] * 2,
            [VMEM] * (len(blocks) + 1),
            4 * height * rhs.shape[0] * columns,
            *blocks,
            rhs,
        )
        distance = 1
        while columns > width:
            came = traded(send, "site", distance)
            columns //= 2
            distance *= 2
            keep, send = local_call(
                combine_kernel,
                "combine",
                [
                    jax.ShapeDtypeStruct((height, columns), jnp.float32),
                    jax.ShapeDtypeStruct((height, columns), jnp.bfloat16),
                ],
                [VMEM] * 2,
                0,
                keep,
                came,
            )
        return [keep, traded(send, "site", distance)]

    near = group_of(below + [packed])
    last = group_of(above)
    band = (2 * reach + 1) * vrows
    gathered = local_call(
        gather_kernel,
        "gather",
        jax.ShapeDtypeStruct((width, band - last[0].shape[0]), jnp.float32),
        [VMEM] * len(near),
        0,
        *near,
    )
    out = local_call(
        finish_kernel,
        "finish",
        jax.ShapeDtypeStruct((width, band), jnp.float32),
        [VMEM] * 3,
        0,
        gathered,
        *last,
    )
    return out.reshape(2, nph, rows, band)


def solution(mesh):
    placed = (P(None, ("grp", "mode"), None, "site"), P(None, ("grp", "mode"), None, "site"), P())
    return jax.shard_map(
        shards,
        mesh=mesh,
        in_specs=placed,
        out_specs=P(None, None, ("grp", "mode", "site"), None),
        check_vma=False,
    )
```

```python
import jax
import jax.numpy as jnp
import numpy as np
from jax import lax
from jax.experimental import pallas as pl
from jax.experimental.pallas import tpu as pltpu
from jax.sharding import PartitionSpec as P


LAT = 96
REACH = 4
SPINS = 4
SIGNS = (-1.0, 1.0, 1.0, -1.0)


def shifted(value, axis, steps):
    count = lax.axis_size(axis)
    pairs = [(source, (source + steps) % count) for source in range(count)]
    return lax.ppermute(value, axis, pairs)


def traded(value, axis, distance):
    count = lax.axis_size(axis)
    return lax.ppermute(value, axis, [(source, source ^ distance) for source in range(count)])


def stages(count):
    return [(2 << stage) - 1 for stage in range(count.bit_length() - 1)]


def slot_order(distances):
    order = [0]
    for distance in reversed(distances):
        order = order + [slot ^ distance for slot in order]
    return order


def make_phase(momenta, first, count):
    index = first + jnp.arange(count, dtype=jnp.int32)
    xcoord = index % LAT
    ycoord = index // LAT % LAT
    zcoord = index // (LAT * LAT)
    total = (
        momenta[:, 0:1] * xcoord[None, :]
        + momenta[:, 1:2] * ycoord[None, :]
        + momenta[:, 2:3] * zcoord[None, :]
    )
    wound = total % LAT
    angle = -2.0 * np.pi / LAT * wound.astype(jnp.float32)
    return (jnp.cos(angle), jnp.sin(angle))


def prepare_kernel(slots, nph, rows, owner_ref, w_ref, cos_ref, sin_ref, b_ref):
    wrows = w_ref.shape[3]
    sites = w_ref.shape[2]
    nsc = w_ref.shape[1]
    colours = nsc // SPINS
    wide = nph * rows
    lane = lax.broadcasted_iota(jnp.int32, (wrows, wide), 1) % rows
    line = lax.broadcasted_iota(jnp.int32, (wrows, wide), 0)
    picks = jnp.concatenate(
        [(line == lane + owner_ref[slot] * rows).astype(jnp.float32) for slot in range(slots)], axis=1
    ).astype(jnp.bfloat16)
    cosine = cos_ref[...]
    sine = sin_ref[...]
    for sc in range(nsc):
        spin, colour = divmod(sc, colours)
        other = (SPINS - 1 - spin) * colours + colour
        c, s = (cosine, sine) if SIGNS[SPINS - 1 - spin] > 0 else (-cosine, -sine)
        both = jnp.concatenate([w_ref[0, other], w_ref[1, other]], axis=0)
        spread = jnp.dot(both, picks, preferred_element_type=jnp.float32)
        for slot in range(slots):
            wreal = spread[:sites, slot * wide : (slot + 1) * wide]
            wimag = spread[sites:, slot * wide : (slot + 1) * wide]
            areal = wreal * c + wimag * s
            aimag = wreal * s - wimag * c
            low = areal.astype(jnp.bfloat16)
            high = aimag.astype(jnp.bfloat16)
            top = slice(sc * 2 * sites, (sc * 2 + 1) * sites)
            bottom = slice((sc * 2 + 1) * sites, (sc * 2 + 2) * sites)
            first = slice((2 * slot) * wide, (2 * slot + 1) * wide)
            second = slice((2 * slot + 1) * wide, (2 * slot + 2) * wide)
            b_ref[top, first] = low
            b_ref[bottom, first] = (-aimag).astype(jnp.bfloat16)
            b_ref[top, second] = high
            b_ref[bottom, second] = low


def contract_kernel(slots, *refs):
    *blocks, b_ref, out_ref = refs
    lhs = jnp.concatenate(
        [jnp.concatenate([block[sc] for sc in range(block.shape[0])], axis=1) for block in blocks], axis=0
    )
    width = out_ref.shape[1] // len(slots)
    for at, slot in enumerate(slots):
        rhs = b_ref[:, slot * width : (slot + 1) * width]
        part = jnp.dot(lhs, rhs, preferred_element_type=jnp.float32)
        out_ref[:, at * width : (at + 1) * width] = part.astype(out_ref.dtype)


def total_of(kept, came):
    return kept[...] + came[...].astype(jnp.float32)


def combine_kernel(kept_ref, came_ref, keep_ref, send_ref):
    total = total_of(kept_ref, came_ref)
    width = keep_ref.shape[1]
    send_ref[...] = total[:, width:].astype(send_ref.dtype)
    keep_ref[...] = total[:, :width]


def gather_kernel(*refs):
    *parts, out_ref = refs
    sums = [total_of(*parts[at : at + 2]) for at in range(0, len(parts), 2)]
    out_ref[...] = jnp.concatenate(sums, axis=0).T


def finish_kernel(near_ref, kept_ref, came_ref, out_ref):
    out_ref[...] = jnp.concatenate([near_ref[...], total_of(kept_ref, came_ref).T], axis=1)


VMEM = pl.BlockSpec(memory_space=pltpu.VMEM)
GRANT = 16 << 20


def local_call(body, out_shape, in_specs, flops, *operands):
    outs = out_shape if isinstance(out_shape, list) else [out_shape]
    moved = sum(int(np.prod(x.shape)) * x.dtype.itemsize for x in [*operands, *outs])
    return pl.pallas_call(
        body,
        out_shape=out_shape,
        in_specs=in_specs,
        out_specs=[VMEM] * len(outs) if isinstance(out_shape, list) else VMEM,
        cost_estimate=pl.CostEstimate(flops=flops, bytes_accessed=moved, transcendentals=0),
        compiler_params=pltpu.CompilerParams(vmem_limit_bytes=GRANT),
    )(*operands)


def shards(w_modes, v_modes, momenta):
    wrows = w_modes.shape[1]
    nsc = w_modes.shape[2]
    sites = w_modes.shape[3]
    vrows = v_modes.shape[1]
    nph = momenta.shape[0]
    nmode = lax.axis_size("mode")
    nsite = lax.axis_size("site")
    reach = min(REACH, (nmode - 1) // 2)
    rows = wrows // nsite
    width = 2 * nph * rows
    me = lax.axis_index("site")

    vt = jnp.transpose(v_modes, (0, 2, 1, 3))
    packed = jnp.concatenate([vt[0], vt[1]], axis=-1)
    below = [shifted(packed, "mode", step) for step in range(reach, 0, -1)]
    above = [shifted(packed, "mode", -step) for step in range(1, reach + 1)]

    cosine, sine = make_phase(momenta, me * sites, sites)
    cosine = jnp.repeat(cosine.T, rows, axis=1)
    sine = jnp.repeat(sine.T, rows, axis=1)
    owners = jnp.stack([me ^ slot for slot in range(nsite)]).astype(jnp.int32)
    wt = jnp.transpose(w_modes, (0, 2, 3, 1))
    rhs = local_call(
        lambda *refs: prepare_kernel(nsite, nph, rows, *refs),
        jax.ShapeDtypeStruct((nsc * 2 * sites, nsite * width), jnp.bfloat16),
        [pl.BlockSpec(memory_space=pltpu.SMEM), VMEM, VMEM, VMEM],
        2 * nsc * 2 * sites * wrows * nsite * nph * rows,
        owners,
        wt,
        cosine,
        sine,
    )

    def group_of(blocks, distances):
        height = len(blocks) * vrows
        order = slot_order(distances)
        half = nsite // 2

        def sent_as(distance):
            return jnp.float32 if distance == 1 else jnp.bfloat16

        def contract(slots, kind):
            return local_call(
                lambda *refs: contract_kernel(slots, *refs),
                jax.ShapeDtypeStruct((height, half * width), kind),
                [VMEM] * (len(blocks) + 1),
                2 * height * rhs.shape[0] * half * width,
                *blocks,
                rhs,
            )

        send = contract(order[half:], sent_as(distances[0]))
        keep = contract(order[:half], jnp.float32)
        for stage, distance in enumerate(distances):
            came = traded(send, "site", distance)
            if stage + 1 == len(distances):
                return [keep, came]
            columns = keep.shape[1] // 2
            keep, send = local_call(
                combine_kernel,
                [
                    jax.ShapeDtypeStruct((height, columns), jnp.float32),
                    jax.ShapeDtypeStruct((height, columns), sent_as(distances[stage + 1])),
                ],
                [VMEM] * 2,
                0,
                keep,
                came,
            )

    near = group_of(below + [packed], stages(nsite)[::-1])
    last = group_of(above, stages(nsite))
    band = (2 * reach + 1) * vrows
    gathered = local_call(
        gather_kernel, jax.ShapeDtypeStruct((width, band - last[0].shape[0]), jnp.float32), [VMEM] * len(near), 0, *near
    )
    out = local_call(finish_kernel, jax.ShapeDtypeStruct((width, band), jnp.float32), [VMEM] * 3, 0, gathered, *last)
    return out.reshape(2, nph, rows, band)


def solution(mesh):
    placed = (P(None, ("grp", "mode"), None, "site"), P(None, ("grp", "mode"), None, "site"), P())

    return jax.shard_map(
        shards,
        mesh=mesh,
        in_specs=placed,
        out_specs=P(None, None, ("grp", "mode", "site"), None),
        check_vma=False,
    )
```
